32 devices in a mesh: dp: 16 (over z, y, x), tensor: 2 (over core).
Axes of the slice: x: 2, y: 2, z: 4, core: 2. Of those that a mesh axis runs over, the one named last changes fastest.
Arguments:
- src: bfloat16 [16, 1024, 1024], P('dp', 'tensor'), may hold values from -6 to 6
- tgt: bfloat16 [16, 1024, 1024], P('dp', 'tensor'), may hold values from -6 to 6
- src_len: int32 [16], P('dp'), may hold values from 256 to 1024, as said below
- tgt_len: int32 [16], P('dp'), may hold values from 256 to 1024, as said below
- enc_qkv: bfloat16 [3, 1024, 1024], P(None, None, 'tensor'), may hold values from -0.1875 to 0.1875
- enc_out_w: bfloat16 [1024, 1024], P('tensor'), may hold values from -1.5 to 1.5
- enc_ffn_in: bfloat16 [1024, 4096], P(None, 'tensor'), may hold values from -0.1875 to 0.1875
- enc_ffn_out: bfloat16 [4096, 1024], P('tensor'), may hold values from -0.09375 to 0.09375
- enc_gain: float32 [3, 1024], replicated, may hold values from 0.25 to 1.75
- enc_bias: float32 [3, 1024], replicated, may hold values from -1.5 to 1.5
- dec_qkv: bfloat16 [3, 1024, 1024], P(None, None, 'tensor'), may hold values from -0.1875 to 0.1875
- dec_self_out: bfloat16 [1024, 1024], P('tensor'), may hold values from -1.5 to 1.5
- dec_cross: bfloat16 [3, 1024, 1024], P(None, None, 'tensor'), may hold values from -0.1875 to 0.1875
- dec_cross_out: bfloat16 [1024, 1024], P('tensor'), may hold values from -1.5 to 1.5
- dec_ffn_in: bfloat16 [1024, 4096], P(None, 'tensor'), may hold values from -0.1875 to 0.1875
- dec_ffn_out: bfloat16 [4096, 1024], P('tensor'), may hold values from -0.09375 to 0.09375
- dec_gain: float32 [4, 1024], replicated, may hold values from 0.25 to 1.75
- dec_bias: float32 [4, 1024], replicated, may hold values from -1.5 to 1.5
- enc_cot: bfloat16 [16, 1024, 1024], P('dp', 'tensor'), may hold values from -6 to 6
- dec_cot: bfloat16 [16, 1024, 1024], P('dp', 'tensor'), may hold values from -6 to 6
Outputs:
- enc_out: bfloat16 [16, 1024, 1024], P('dp', 'tensor')
- dec_out: bfloat16 [16, 1024, 1024], P('dp', 'tensor')
- grad_src: float32 [16, 1024, 1024], P('dp', 'tensor')
- grad_tgt: float32 [16, 1024, 1024], P('dp', 'tensor')
- enc_qkv_grad: float32 [3, 1024, 1024], P(None, None, 'tensor')
- enc_out_w_grad: float32 [1024, 1024], P('tensor')
- enc_ffn_in_grad: float32 [1024, 4096], P(None, 'tensor')
- enc_ffn_out_grad: float32 [4096, 1024], P('tensor')
- enc_gain_grad: float32 [3, 1024], replicated
- enc_bias_grad: float32 [3, 1024], replicated
- dec_qkv_grad: float32 [3, 1024, 1024], P(None, None, 'tensor')
- dec_self_out_grad: float32 [1024, 1024], P('tensor')
- dec_cross_grad: float32 [3, 1024, 1024], P(None, None, 'tensor')
- dec_cross_out_grad: float32 [1024, 1024], P('tensor')
- dec_ffn_in_grad: float32 [1024, 4096], P(None, 'tensor')
- dec_ffn_out_grad: float32 [4096, 1024], P('tensor')
- dec_gain_grad: float32 [4, 1024], replicated
- dec_bias_grad: float32 [4, 1024], replicated
The draws below stay inside these ranges and needn't reach their ends.
Inputs may be any that keep to these rules, and one draw needn't show every extreme that they name: The first src_len[b] positions of pair b's source are filled and the rest is padding; in every draw some pair has a full source of 1024. `tgt_len`: likewise for the target positions; in every draw some pair has a full target of 1024.
All inputs are finite; a program needn't handle non-finite values.
Results may differ from the reference program's by a relative error of at most 0.022.
Values may be sent and summed in bfloat16 or wider, within the bound.
No kernel may reach another device: no remote copies, remote signals or barrier semaphores. Data moves between devices by JAX's collectives and lax.ppermute only.
A program may use at most 448 MiB of HBM per device.

```python
import jax
import jax.numpy as jnp
from jax import lax

D = 1024
HEADS = 16
HEAD_DIM = 64
FF = 4096
SEQ = 1024
BATCH = 16
QBLK = 512


def draw_lengths(key):
    first, second = jax.random.split(key)
    counts = jax.random.randint(first, (BATCH,), SEQ // 4, SEQ + 1)
    chosen = jax.random.randint(second, (), 0, BATCH)
    return counts.at[chosen].set(SEQ).astype(jnp.int32)


def draw_src_len(key, part):
    return draw_lengths(jax.random.fold_in(key, 11))


def draw_tgt_len(key, part):
    return draw_lengths(jax.random.fold_in(key, 23))


def block_levels(stream_key, extent, shards, low, largest):
    level = 1.0
    for axis_at, blocks in shards:
        heights = jax.random.uniform(jax.random.fold_in(jax.random.fold_in(stream_key, 6), axis_at), (blocks,), jnp.float32, low / len(shards), largest / len(shards))
        level = level * jnp.repeat(jnp.exp(heights), extent[axis_at] // blocks).reshape((-1,) + (1,) * (len(extent) - 1 - axis_at))
    return level


def gaussian(own_key, extent, scale, most, pieces=(), kind=jnp.bfloat16):
    entries = jax.random.normal(own_key, extent, jnp.float32) * scale
    if len(pieces) > 0:
        entries = block_levels(own_key, extent, pieces, -0.22, 0.18) * entries
    return jnp.clip(entries, min=-most, max=most).astype(kind)


def setup_inputs(seed: int = 0) -> dict:
    seeds = jax.random.split(jax.random.key(seed), 21)
    src = gaussian(seeds[0], (BATCH, SEQ, D), 1.0, 6.0, ((0, 16), (1, 2)))
    tgt = gaussian(seeds[1], (BATCH, SEQ, D), 1.0, 6.0, ((0, 16), (1, 2)))
    src_len = draw_src_len(jax.random.fold_in(seeds[20], 71), 0)
    tgt_len = draw_tgt_len(jax.random.fold_in(seeds[20], 71), 0)
    enc_qkv = gaussian(seeds[4], (3, D, HEADS * HEAD_DIM), D ** -0.5, 0.1875, ((2, 2),))
    enc_out_w = gaussian(seeds[5], (HEADS * HEAD_DIM, D), (max(HEADS * HEAD_DIM // 64, 1)) ** -0.5, 1.5, ((0, 2),))
    enc_ffn_in = gaussian(seeds[6], (D, FF), D ** -0.5, 0.1875, ((1, 2),))
    enc_ffn_out = gaussian(seeds[7], (FF, D), FF ** -0.5, 0.09375, ((0, 2),))
    enc_gain = jnp.clip(1.0 + 0.15 * jax.random.normal(seeds[8], (3, D), jnp.float32), 0.25, 1.75)
    enc_bias = gaussian(seeds[9], (3, D), 0.3, 1.5, (), jnp.float32)
    dec_qkv = gaussian(seeds[10], (3, D, HEADS * HEAD_DIM), D ** -0.5, 0.1875, ((2, 2),))
    dec_self_out = gaussian(seeds[11], (HEADS * HEAD_DIM, D), (max(HEADS * HEAD_DIM // 64, 1)) ** -0.5, 1.5, ((0, 2),))
    dec_cross = gaussian(seeds[12], (3, D, HEADS * HEAD_DIM), D ** -0.5, 0.1875, ((2, 2),))
    dec_cross_out = gaussian(seeds[13], (HEADS * HEAD_DIM, D), (max(HEADS * HEAD_DIM // 64, 1)) ** -0.5, 1.5, ((0, 2),))
    dec_ffn_in = gaussian(seeds[14], (D, FF), D ** -0.5, 0.1875, ((1, 2),))
    dec_ffn_out = gaussian(seeds[15], (FF, D), FF ** -0.5, 0.09375, ((0, 2),))
    dec_gain = jnp.clip(1.0 + 0.15 * jax.random.normal(seeds[16], (4, D), jnp.float32), 0.25, 1.75)
    dec_bias = gaussian(seeds[17], (4, D), 0.3, 1.5, (), jnp.float32)
    enc_cot = gaussian(seeds[18], (BATCH, SEQ, D), 1.0, 6.0, ((0, 16), (1, 2)))
    dec_cot = gaussian(seeds[19], (BATCH, SEQ, D), 1.0, 6.0, ((0, 16), (1, 2)))
    return {"src": src, "tgt": tgt, "src_len": src_len, "tgt_len": tgt_len, "enc_qkv": enc_qkv, "enc_out_w": enc_out_w, "enc_ffn_in": enc_ffn_in, "enc_ffn_out": enc_ffn_out, "enc_gain": enc_gain, "enc_bias": enc_bias, "dec_qkv": dec_qkv, "dec_self_out": dec_self_out, "dec_cross": dec_cross, "dec_cross_out": dec_cross_out, "dec_ffn_in": dec_ffn_in, "dec_ffn_out": dec_ffn_out, "dec_gain": dec_gain, "dec_bias": dec_bias, "enc_cot": enc_cot, "dec_cot": dec_cot}


epsilon = 1e-05
highest = lax.Precision.HIGHEST

@jax.custom_vjp
def low(v):
    return lax.optimization_barrier(v.astype(jnp.bfloat16)).astype(jnp.float32)

@jax.custom_vjp
def low_back(v):
    return v

def low_keep(v):
    return (low(v), None)

def low_pass(kept, grad):
    return (grad,)

def back_keep(v):
    return (v, None)

def back_low(kept, grad):
    return (low(grad),)
low.defvjp(low_keep, low_pass)
low_back.defvjp(back_keep, back_low)

def round_both(value):
    return low_back(low(value))

def matmul_high(left, right):
    return jnp.dot(left, right, precision=highest)

def layer_norm(hidden, gain, shift):
    center = hidden - lax.optimization_barrier(jnp.mean(hidden, axis=-1, keepdims=True))
    variance = lax.optimization_barrier(jnp.mean(center * center, axis=-1, keepdims=True))
    return center * lax.rsqrt(variance + epsilon) * gain + shift

def split_heads(value):
    return value.reshape(SEQ, HEADS, HEAD_DIM).transpose(1, 0, 2)

def attend(query_in, memory_in, w_query, w_key, w_value, w_out, key_len, causal):
    queries = split_heads(round_both(matmul_high(query_in, w_query)))
    keys = split_heads(round_both(matmul_high(memory_in, w_key)))
    values = split_heads(round_both(matmul_high(memory_in, w_value)))
    key_pos = jnp.arange(SEQ)
    valid = key_pos < key_len
    block_count = SEQ // QBLK
    query_blocks = queries.reshape(HEADS, block_count, QBLK, HEAD_DIM).transpose(1, 0, 2, 3)
    starts = jnp.arange(block_count) * QBLK

    def block_fn(item):
        query_block, start = item
        raw = jnp.einsum('hqd,hkd->hqk', query_block, keys, precision=highest)
        scores = low_back(raw) * HEAD_DIM ** (-0.5)
        allowed = valid[None, :]
        if causal:
            query_pos = start + jnp.arange(QBLK)
            allowed = allowed & (key_pos[None, :] <= query_pos[:, None])
        scores = jnp.where(allowed[None], scores, -1e+30)
        row_top = lax.optimization_barrier(jnp.max(scores, axis=-1, keepdims=True))
        exp_scores = jnp.exp(scores - row_top)
        soft_weights = exp_scores / lax.optimization_barrier(jnp.sum(exp_scores, axis=-1, keepdims=True))
        return jnp.einsum('hqk,hkd->hqd', low(soft_weights), values, precision=highest)
    context = lax.map(jax.checkpoint(block_fn), (query_blocks, starts))
    context = round_both(context.transpose(0, 2, 1, 3).reshape(SEQ, HEADS * HEAD_DIM))
    return low_back(matmul_high(context, w_out))

def feed_forward(rows, w_in, w_out):
    zed = low_back(matmul_high(rows, w_in))
    unit = round_both(jax.nn.gelu(zed, approximate=False))
    return low_back(matmul_high(unit, w_out))

def pair_forward(params, source, target, src_count, tgt_count):
    eqkv, e_out, e_in_ff, e_out_ff, e_gain, e_bias, dqkv, d_self, d_cross, d_cross_out, d_in_ff, d_out_ff, d_gain, d_bias = params
    a_one = low(layer_norm(source, e_gain[0], e_bias[0]))
    h_one = source + attend(a_one, a_one, eqkv[0], eqkv[1], eqkv[2], e_out, src_count, False)
    a_two = low(layer_norm(h_one, e_gain[1], e_bias[1]))
    h_two = h_one + feed_forward(a_two, e_in_ff, e_out_ff)
    memory = low(layer_norm(h_two, e_gain[2], e_bias[2]))
    b_one = low(layer_norm(target, d_gain[0], d_bias[0]))
    r_one = target + attend(b_one, b_one, dqkv[0], dqkv[1], dqkv[2], d_self, tgt_count, True)
    b_two = low(layer_norm(r_one, d_gain[1], d_bias[1]))
    r_two = r_one + attend(b_two, memory, d_cross[0], d_cross[1], d_cross[2], d_cross_out, src_count, False)
    b_three = low(layer_norm(r_two, d_gain[2], d_bias[2]))
    r_three = r_two + feed_forward(b_three, d_in_ff, d_out_ff)
    return (memory, layer_norm(r_three, d_gain[3], d_bias[3]))

def reference(src, tgt, src_len, tgt_len, enc_qkv, enc_out_w, enc_ffn_in, enc_ffn_out, enc_gain, enc_bias, dec_qkv, dec_self_out, dec_cross, dec_cross_out, dec_ffn_in, dec_ffn_out, dec_gain, dec_bias, enc_cot, dec_cot):
    params = tuple((w.astype(jnp.float32) for w in (enc_qkv, enc_out_w, enc_ffn_in, enc_ffn_out, enc_gain, enc_bias, dec_qkv, dec_self_out, dec_cross, dec_cross_out, dec_ffn_in, dec_ffn_out, dec_gain, dec_bias)))

    def step(totals, item):
        s_in, t_in, s_count, t_count, e_grad, d_grad = item

        def run(prm, s_val, t_val):
            return pair_forward(prm, s_val, t_val, s_count, t_count)
        (e_val, d_val), pull = jax.vjp(run, params, s_in.astype(jnp.float32), t_in.astype(jnp.float32))
        g_params, g_src, g_tgt = pull((e_grad.astype(jnp.float32), d_grad.astype(jnp.float32)))
        totals = jax.tree.map(jnp.add, totals, g_params)
        return (totals, (e_val.astype(jnp.bfloat16), d_val.astype(jnp.bfloat16), g_src, g_tgt))
    zeros = jax.tree.map(jnp.zeros_like, params)
    totals, outputs = lax.scan(step, zeros, (src, tgt, src_len, tgt_len, enc_cot, dec_cot))
    return (outputs[0], outputs[1], outputs[2], outputs[3], totals[0], totals[1], totals[2], totals[3], totals[4], totals[5], totals[6], totals[7], totals[8], totals[9], totals[10], totals[11], totals[12], totals[13])
```

```python
import math
from functools import partial

import jax
import jax.numpy as jnp
from jax import lax
from jax.experimental import pallas as pl
from jax.experimental.pallas import tpu as pltpu
from jax.sharding import PartitionSpec as P

HEAD_DIM = 64
PAIR = 2 * HEAD_DIM
QBLK = 512
QBLK_BACK = 512
BF = jnp.bfloat16
F32 = jnp.float32

epsilon = 1e-05
root_half = 1.0 / math.sqrt(2.0)
root_two_pi = 1.0 / math.sqrt(2.0 * math.pi)
score_scale = HEAD_DIM**-0.5
log2_scale = score_scale * math.log2(math.e)
NEG = -1e30


def norm_forward(hidden, gain, shift):
    center = hidden - jnp.mean(hidden, axis=-1, keepdims=True)
    inverse = lax.rsqrt(jnp.mean(center * center, axis=-1, keepdims=True) + epsilon)
    normed = center * inverse
    return (normed * gain + shift, normed, inverse)


def norm_backward(grad, normed, inverse, gain):
    scaled = grad * gain
    inner = (
        scaled
        - jnp.mean(scaled, axis=-1, keepdims=True)
        - normed * jnp.mean(scaled * normed, axis=-1, keepdims=True)
    )
    return (inverse * inner, jnp.sum(grad * normed, axis=0), jnp.sum(grad, axis=0))


def gelu_value(zed):
    return 0.5 * zed * (1.0 + lax.erf(zed * root_half))


def gelu_slope(zed):
    return 0.5 * (1.0 + lax.erf(zed * root_half)) + zed * jnp.exp(-0.5 * zed * zed) * root_two_pi


def dot(left, right, left_dim, right_dim):
    return lax.dot_general(
        left, right, (((left_dim,), (right_dim,)), ((), ())), preferred_element_type=F32
    )


def project(left, weight):
    return dot(left, weight, 1, 0)


def back_project(grad, weight):
    return dot(grad, weight, 1, 1)


def weight_grad(left, grad):
    return dot(left, grad, 0, 0)


def swap(value):
    return lax.ppermute(value, "tensor", [(0, 1), (1, 0)])


def spread(rows):
    if lax.axis_size("tensor") == 2:
        return jnp.concatenate([rows, swap(rows)], axis=0)
    return lax.all_gather(rows, "tensor", axis=0, tiled=True)


def collect(partial_rows):
    if lax.axis_size("tensor") == 2:
        half = partial_rows.shape[0] // 2
        return partial_rows[:half] + swap(partial_rows[half:].astype(BF)).astype(F32)
    return lax.psum_scatter(
        partial_rows.astype(BF), "tensor", scatter_dimension=0, tiled=True
    ).astype(F32)


def lane_of(shape):
    return lax.broadcasted_iota(jnp.int32, shape, 1)


def head_lanes(value, head, spare):
    lane = lane_of(value.shape)
    mine = (lane >= head * HEAD_DIM) & (lane < (head + 1) * HEAD_DIM)
    slot = lane == (1 - head) * HEAD_DIM
    return jnp.where(mine, value, jnp.where(slot, spare, 0.0)).astype(BF)


def positions(count, axis, shape, start, shift, total):
    pos = lax.broadcasted_iota(jnp.int32, shape, axis) + (start + shift)
    return jnp.where(pos >= total, pos - total, pos)


def masked_keys(meta_ref, k_ref, kh_ref):
    total = k_ref.shape[0]
    keys = k_ref[...].astype(F32)
    pos = positions(total, 0, keys.shape, 0, meta_ref[0], total)
    spare = jnp.where(pos < meta_ref[1], 0.0, NEG)
    for head in range(2):
        kh_ref[head] = head_lanes(keys, head, spare)


def scores_of(meta_ref, kh_ref, head, query_f32, start, causal):
    total = kh_ref.shape[1]
    scores = dot(kh_ref[head], head_lanes(query_f32, head, 1.0), 1, 1)
    if causal:
        shape = scores.shape
        key_pos = positions(total, 0, (total, 1), 0, meta_ref[0], total)
        query_pos = positions(shape[1], 1, (1, shape[1]), start, meta_ref[0], total)
        scores = jnp.where(key_pos <= query_pos, scores, NEG)
    return scores


def forward_kernel(meta_ref, q_ref, k_ref, v_ref, ctx_ref, lse_ref, kh_ref, vt_ref, *, causal):
    block = pl.program_id(1)

    @pl.when(block == 0)
    def _():
        masked_keys(meta_ref, k_ref, kh_ref)
        vt_ref[...] = v_ref[...].astype(F32).T.astype(BF)

    query = q_ref[...].astype(F32)
    start = block * q_ref.shape[0]
    parts = []
    for head in range(2):
        scores = scores_of(meta_ref, kh_ref, head, query, start, causal)
        top = jnp.max(scores, axis=0, keepdims=True) * log2_scale
        weights = jnp.exp2(scores * log2_scale - top)
        total = jnp.sum(weights, axis=0, keepdims=True)
        values = vt_ref[head * HEAD_DIM : (head + 1) * HEAD_DIM, :]
        parts.append(dot(values, weights.astype(BF), 1, 0) / total)
        lse_ref[0, head : head + 1, :] = top + jnp.log2(total)
    ctx_ref[...] = jnp.concatenate(parts, axis=0).T.astype(BF)


def backward_kernel(
    meta_ref,
    q_ref,
    k_ref,
    v_ref,
    do_ref,
    ctx_ref,
    lse_ref,
    dq_ref,
    dk_ref,
    dv_ref,
    kh_ref,
    kt_ref,
    dk_acc,
    dv_acc,
    *,
    causal,
):
    block = pl.program_id(1)

    @pl.when(block == 0)
    def _():
        masked_keys(meta_ref, k_ref, kh_ref)
        kt_ref[...] = k_ref[...].astype(F32).T.astype(BF)
        dk_acc[...] = jnp.zeros_like(dk_acc)
        dv_acc[...] = jnp.zeros_like(dv_acc)

    query = q_ref[...].astype(F32)
    grad = do_ref[...].astype(F32)
    start = block * q_ref.shape[0]
    products = (grad * ctx_ref[...].astype(F32)).T
    parts = []
    for head in range(2):
        low, high = head * HEAD_DIM, (head + 1) * HEAD_DIM
        scores = scores_of(meta_ref, kh_ref, head, query, start, causal)
        soft = jnp.exp2(scores * log2_scale - lse_ref[0, head : head + 1, :])
        grad_head = head_lanes(grad, head, 0.0)
        row_dot = jnp.sum(products[low:high, :], axis=0, keepdims=True)
        grad_soft = dot(v_ref[...], grad_head, 1, 1)
        grad_scores = (soft * (grad_soft - row_dot)).astype(BF)
        dv_acc[...] += dot(soft.astype(BF), grad_head, 1, 0)
        dk_acc[...] += dot(grad_scores, head_lanes(query, head, 0.0), 1, 0)
        parts.append(dot(kt_ref[low:high, :], grad_scores, 1, 0))
    dq_ref[...] = (jnp.concatenate(parts, axis=0).T * score_scale).astype(BF)

    @pl.when(block == pl.num_programs(1) - 1)
    def _():
        dk_ref[...] = (dk_acc[...] * score_scale).astype(BF)
        dv_ref[...] = dv_acc[...].astype(BF)


def row_spec(rows):
    return pl.BlockSpec((rows, PAIR), lambda pair, block, meta: (block, pair))


def whole_spec(rows):
    return pl.BlockSpec((rows, PAIR), lambda pair, block, meta: (0, pair))


def lse_spec(rows):
    return pl.BlockSpec((1, 2, rows), lambda pair, block, meta: (pair, 0, block))


def attend_forward(meta, queries, keys, values, causal):
    total, width = queries.shape
    pairs = width // PAIR
    rows = min(QBLK, total)
    return pl.pallas_call(
        partial(forward_kernel, causal=causal),
        grid_spec=pltpu.PrefetchScalarGridSpec(
            num_scalar_prefetch=1,
            grid=(pairs, total // rows),
            in_specs=[row_spec(rows), whole_spec(total), whole_spec(total)],
            out_specs=[row_spec(rows), lse_spec(rows)],
            scratch_shapes=[pltpu.VMEM((2, total, PAIR), BF), pltpu.VMEM((PAIR, total), BF)],
        ),
        out_shape=[
            jax.ShapeDtypeStruct((total, width), BF),
            jax.ShapeDtypeStruct((pairs, 2, total), F32),
        ],
        name="attend_forward",
    )(meta, queries, keys, values)


def attend_backward(meta, queries, keys, values, grad, context, log_sums, causal):
    total, width = queries.shape
    pairs = width // PAIR
    rows = min(QBLK_BACK, total)
    return pl.pallas_call(
        partial(backward_kernel, causal=causal),
        grid_spec=pltpu.PrefetchScalarGridSpec(
            num_scalar_prefetch=1,
            grid=(pairs, total // rows),
            in_specs=[
                row_spec(rows),
                whole_spec(total),
                whole_spec(total),
                row_spec(rows),
                row_spec(rows),
                lse_spec(rows),
            ],
            out_specs=[row_spec(rows), whole_spec(total), whole_spec(total)],
            scratch_shapes=[
                pltpu.VMEM((2, total, PAIR), BF),
                pltpu.VMEM((PAIR, total), BF),
                pltpu.VMEM((total, PAIR), F32),
                pltpu.VMEM((total, PAIR), F32),
            ],
        ),
        out_shape=[jax.ShapeDtypeStruct((total, width), BF)] * 3,
        name="attend_backward",
    )(meta, queries, keys, values, grad, context, log_sums)


def attention_forward(query_in, memory_in, w_qkv, w_out, meta, causal):
    queries = project(query_in, w_qkv[0]).astype(BF)
    keys = project(memory_in, w_qkv[1]).astype(BF)
    values = project(memory_in, w_qkv[2]).astype(BF)
    context, log_sums = attend_forward(meta, queries, keys, values, causal)
    return (collect(project(context, w_out)), (queries, keys, values, context, log_sums))


def attention_backward(grad_out, query_in, memory_in, w_qkv, w_out, kept, meta, causal):
    queries, keys, values, context, log_sums = kept
    grad_full = spread(grad_out.astype(BF))
    grad_context = back_project(grad_full, w_out).astype(BF)
    grad_w_out = weight_grad(grad_full, context).astype(BF)
    grad_q, grad_k, grad_v = attend_backward(
        meta, queries, keys, values, grad_context, context, log_sums, causal
    )
    first = jnp.concatenate(
        [weight_grad(query_in, grad_q).astype(BF), weight_grad(memory_in, grad_k).astype(BF)]
    )
    second = jnp.concatenate([weight_grad(memory_in, grad_v).astype(BF), grad_w_out])
    from_query = back_project(grad_q, w_qkv[0])
    from_memory = back_project(grad_k, w_qkv[1]) + back_project(grad_v, w_qkv[2])
    return ((first, second), from_query, from_memory)


def ffn_forward(normed_rows, w_in, w_out):
    rows_full = spread(normed_rows)
    zed = project(rows_full, w_in)
    unit = gelu_value(zed).astype(BF)
    result = collect(project(unit, w_out))
    return (result, (rows_full, zed, unit, w_in, w_out))


def ffn_backward(grad_out, kept):
    rows, zed, unit, w_in, w_out = kept
    grad_full = spread(grad_out.astype(BF))
    grad_w_out = weight_grad(unit, grad_full).astype(BF)
    grad_unit = back_project(grad_full, w_out).astype(BF)
    grad_zed = (grad_unit.astype(F32) * gelu_slope(zed)).astype(BF)
    grad_w_in = weight_grad(rows, grad_zed).astype(BF)
    grad_input = collect(back_project(grad_zed, w_in))
    return (grad_input, (grad_w_in, grad_w_out))


def copy_out_kernel(index_ref, src_ref, keep_ref, send_ref):
    step = pl.program_id(0)
    half = pl.num_programs(0) // 2

    @pl.when(step < half)
    def _():
        keep_ref[...] = src_ref[...]

    @pl.when(step >= half)
    def _():
        send_ref[...] = src_ref[...]


def copy_in_kernel(index_ref, near_ref, far_ref, out_ref):
    step = pl.program_id(0)
    half = pl.num_programs(0) // 2

    @pl.when(step < half)
    def _():
        out_ref[...] = near_ref[...].astype(F32)

    @pl.when(step >= half)
    def _():
        out_ref[...] = far_ref[...].astype(F32)


def chunk_specs(count, rows, cols):
    half = count // 2
    block = (1, rows, cols)
    whole = pl.BlockSpec(block, lambda step, index: (step ^ index[0], 0, 0))
    near = pl.BlockSpec(block, lambda step, index: (jnp.minimum(step, half - 1), 0, 0))
    far = pl.BlockSpec(block, lambda step, index: (jnp.maximum(step - half, 0), 0, 0))
    return (whole, near, far)


def partner(value, bit):
    count = lax.axis_size("dp")
    return lax.ppermute(value, "dp", [(at, at ^ (1 << bit)) for at in range(count)])


def sum_over_pairs(value, first_bits):
    count = lax.axis_size("dp")
    levels = count.bit_length() - 1
    order = list(first_bits) + [bit for bit in range(levels) if bit not in first_bits]
    place = lax.axis_index("dp")
    index = jnp.zeros((), jnp.int32)
    for bit in order:
        index = index * 2 + ((place >> bit) & 1)
    index = index[None]
    rows = value.shape[0] // count
    cols = value.shape[1]
    half = count // 2
    whole, near, far = chunk_specs(count, rows, cols)
    keep, send = pl.pallas_call(
        copy_out_kernel,
        grid_spec=pltpu.PrefetchScalarGridSpec(
            num_scalar_prefetch=1, grid=(count,), in_specs=[whole], out_specs=[near, far]
        ),
        out_shape=[jax.ShapeDtypeStruct((half, rows, cols), BF)] * 2,
        name="copy_out",
    )(index, value.reshape(count, rows, cols))
    for level, bit in enumerate(order):
        summed = keep + partner(send, bit)
        if level + 1 < levels:
            middle = summed.shape[0] // 2
            keep, send = summed[:middle], summed[middle:]
    for bit in order[:0:-1]:
        summed = jnp.concatenate([summed, partner(summed, bit)])
    other = partner(summed, order[0])
    result = pl.pallas_call(
        copy_in_kernel,
        grid_spec=pltpu.PrefetchScalarGridSpec(
            num_scalar_prefetch=1, grid=(count,), in_specs=[near, far], out_specs=whole
        ),
        out_shape=jax.ShapeDtypeStruct((count, rows, cols), F32),
        name="copy_in",
    )(index, summed, other)
    return result.reshape(value.shape)


def sum_two(pair):
    return (sum_over_pairs(pair[0], (0, 1)), sum_over_pairs(pair[1], (1, 0)))


def sum_everywhere(value):
    for axis in ("tensor", "dp"):
        count = lax.axis_size(axis)
        for bit in range(count.bit_length() - 1):
            value = value + lax.ppermute(
                value, axis, [(at, at ^ (1 << bit)) for at in range(count)]
            )
    return value


def split_attention(pair):
    first, second = pair
    rows = first.shape[0] // 2
    return (
        jnp.concatenate([first, second[:rows]]).reshape(3, rows, first.shape[1]),
        second[rows:].T,
    )


def on_device(
    src,
    tgt,
    src_len,
    tgt_len,
    enc_qkv,
    enc_out_w,
    enc_ffn_in,
    enc_ffn_out,
    enc_gain,
    enc_bias,
    dec_qkv,
    dec_self_out,
    dec_cross,
    dec_cross_out,
    dec_ffn_in,
    dec_ffn_out,
    dec_gain,
    dec_bias,
    enc_cot,
    dec_cot,
):
    if lax.axis_size("tensor") == 2:
        shift = (lax.axis_index("tensor") * src.shape[1]).astype(jnp.int32)
    else:
        shift = jnp.zeros((), jnp.int32)
    src_meta = jnp.stack([shift, src_len[0]])
    tgt_meta = jnp.stack([shift, tgt_len[0]])
    source = src[0].astype(F32)
    target = tgt[0].astype(F32)
    ln_a1, nm_a1, inv_a1 = norm_forward(source, enc_gain[0], enc_bias[0])
    ln_b1, nm_b1, inv_b1 = norm_forward(target, dec_gain[0], dec_bias[0])
    enc_rows = spread(ln_a1.astype(BF))
    dec_rows = spread(ln_b1.astype(BF))
    attn_enc, keep_enc_attn = attention_forward(
        enc_rows, enc_rows, enc_qkv, enc_out_w, src_meta, False
    )
    hidden_one = source + attn_enc
    ln_a2, nm_a2, inv_a2 = norm_forward(hidden_one, enc_gain[1], enc_bias[1])
    ffn_enc, keep_enc_ffn = ffn_forward(ln_a2.astype(BF), enc_ffn_in, enc_ffn_out)
    hidden_two = hidden_one + ffn_enc
    ln_mem, nm_mem, inv_mem = norm_forward(hidden_two, enc_gain[2], enc_bias[2])
    memory = ln_mem.astype(BF)
    attn_self, keep_self = attention_forward(
        dec_rows, dec_rows, dec_qkv, dec_self_out, tgt_meta, True
    )
    resid_one = target + attn_self
    ln_b2, nm_b2, inv_b2 = norm_forward(resid_one, dec_gain[1], dec_bias[1])
    cross_rows = spread(ln_b2.astype(BF))
    memory_rows = spread(memory)
    attn_cross, keep_cross = attention_forward(
        cross_rows, memory_rows, dec_cross, dec_cross_out, src_meta, False
    )
    resid_two = resid_one + attn_cross
    ln_b3, nm_b3, inv_b3 = norm_forward(resid_two, dec_gain[2], dec_bias[2])
    ffn_dec, keep_dec_ffn = ffn_forward(ln_b3.astype(BF), dec_ffn_in, dec_ffn_out)
    resid_three = resid_two + ffn_dec
    ln_final, nm_final, inv_final = norm_forward(resid_three, dec_gain[3], dec_bias[3])
    grad_r3, gain_final, bias_final = norm_backward(
        dec_cot[0].astype(F32), nm_final, inv_final, dec_gain[3]
    )
    grad_b3, dec_ffn_grads = ffn_backward(grad_r3, keep_dec_ffn)
    dec_ffn_sums = sum_two(dec_ffn_grads)
    part_r2, gain_b3, bias_b3 = norm_backward(grad_b3, nm_b3, inv_b3, dec_gain[2])
    grad_r2 = grad_r3 + part_r2
    cross_grads, from_query, from_memory = attention_backward(
        grad_r2,
        cross_rows,
        memory_rows,
        dec_cross,
        dec_cross_out,
        keep_cross,
        src_meta,
        False,
    )
    cross_sums = split_attention(sum_two(cross_grads))
    grad_memory = enc_cot[0].astype(F32) + collect(from_memory)
    grad_h2, gain_mem, bias_mem = norm_backward(grad_memory, nm_mem, inv_mem, enc_gain[2])
    grad_a2, enc_ffn_grads = ffn_backward(grad_h2, keep_enc_ffn)
    enc_ffn_sums = sum_two(enc_ffn_grads)
    part_r1, gain_b2, bias_b2 = norm_backward(collect(from_query), nm_b2, inv_b2, dec_gain[1])
    grad_r1 = grad_r2 + part_r1
    self_grads, self_query, self_memory = attention_backward(
        grad_r1, dec_rows, dec_rows, dec_qkv, dec_self_out, keep_self, tgt_meta, True
    )
    self_sums = split_attention(sum_two(self_grads))
    grad_b1 = collect(self_query + self_memory)
    part_tgt, gain_b1, bias_b1 = norm_backward(grad_b1, nm_b1, inv_b1, dec_gain[0])
    grad_tgt = grad_r1 + part_tgt
    part_h1, gain_a2, bias_a2 = norm_backward(grad_a2, nm_a2, inv_a2, enc_gain[1])
    grad_h1 = grad_h2 + part_h1
    enc_grads, enc_query, enc_memory = attention_backward(
        grad_h1, enc_rows, enc_rows, enc_qkv, enc_out_w, keep_enc_attn, src_meta, False
    )
    enc_sums = split_attention(sum_two(enc_grads))
    grad_a1 = collect(enc_query + enc_memory)
    part_src, gain_a1, bias_a1 = norm_backward(grad_a1, nm_a1, inv_a1, enc_gain[0])
    grad_src = grad_h1 + part_src
    small = sum_everywhere(
        jnp.stack(
            [
                gain_a1,
                gain_a2,
                gain_mem,
                bias_a1,
                bias_a2,
                bias_mem,
                gain_b1,
                gain_b2,
                gain_b3,
                gain_final,
                bias_b1,
                bias_b2,
                bias_b3,
                bias_final,
            ]
        )
    )
    return (
        memory[None],
        ln_final.astype(BF)[None],
        grad_src[None],
        grad_tgt[None],
        enc_sums[0],
        enc_sums[1],
        enc_ffn_sums[0],
        enc_ffn_sums[1],
        small[0:3],
        small[3:6],
        self_sums[0],
        self_sums[1],
        cross_sums[0],
        cross_sums[1],
        dec_ffn_sums[0],
        dec_ffn_sums[1],
        small[6:10],
        small[10:14],
    )


def solution(mesh):
    rows = P("dp", "tensor", None)
    triple = P(None, None, "tensor")
    in_specs = (
        rows,
        rows,
        P("dp"),
        P("dp"),
        triple,
        P("tensor", None),
        P(None, "tensor"),
        P("tensor", None),
        P(),
        P(),
        triple,
        P("tensor", None),
        triple,
        P("tensor", None),
        P(None, "tensor"),
        P("tensor", None),
        P(),
        P(),
        rows,
        rows,
    )
    out_specs = (
        rows,
        rows,
        rows,
        rows,
        triple,
        P("tensor", None),
        P(None, "tensor"),
        P("tensor", None),
        P(),
        P(),
        triple,
        P("tensor", None),
        triple,
        P("tensor", None),
        P(None, "tensor"),
        P("tensor", None),
        P(),
        P(),
    )
    return jax.shard_map(
        on_device, mesh=mesh, in_specs=in_specs, out_specs=out_specs, check_vma=False
    )
```

```python
import math
from functools import partial

import jax
import jax.numpy as jnp
from jax import lax
from jax.experimental import pallas as pl
from jax.experimental.pallas import tpu as pltpu
from jax.sharding import PartitionSpec as P

HEAD_DIM = 64
PAIR = 2 * HEAD_DIM
QBLK = 512
QBLK_BACK = 512
BF = jnp.bfloat16
F32 = jnp.float32

epsilon = 1e-05
root_half = 1.0 / math.sqrt(2.0)
root_two_pi = 1.0 / math.sqrt(2.0 * math.pi)
score_scale = HEAD_DIM**-0.5
log2_scale = score_scale * math.log2(math.e)
NEG = -1e30


def norm_forward(hidden, gain, shift):
    center = hidden - jnp.mean(hidden, axis=-1, keepdims=True)
    inverse = lax.rsqrt(jnp.mean(center * center, axis=-1, keepdims=True) + epsilon)
    normed = center * inverse
    return (normed * gain + shift, normed, inverse)


def norm_backward(grad, normed, inverse, gain):
    scaled = grad * gain
    inner = (
        scaled
        - jnp.mean(scaled, axis=-1, keepdims=True)
        - normed * jnp.mean(scaled * normed, axis=-1, keepdims=True)
    )
    return (inverse * inner, jnp.sum(grad * normed, axis=0), jnp.sum(grad, axis=0))


def gelu_value(zed):
    return 0.5 * zed * (1.0 + lax.erf(zed * root_half))


def gelu_slope(zed):
    return 0.5 * (1.0 + lax.erf(zed * root_half)) + zed * jnp.exp(-0.5 * zed * zed) * root_two_pi


def dot(left, right, left_dim, right_dim):
    return lax.dot_general(
        left, right, (((left_dim,), (right_dim,)), ((), ())), preferred_element_type=F32
    )


def project(left, weight):
    return dot(left, weight, 1, 0)


def back_project(grad, weight):
    return dot(grad, weight, 1, 1)


def weight_grad(left, grad):
    return dot(left, grad, 0, 0)


def swap(value):
    return lax.ppermute(value, "tensor", [(0, 1), (1, 0)])


def spread(rows):
    if lax.axis_size("tensor") == 2:
        return jnp.concatenate([rows, swap(rows)], axis=0)
    return lax.all_gather(rows, "tensor", axis=0, tiled=True)


def collect(partial_rows):
    if lax.axis_size("tensor") == 2:
        half = partial_rows.shape[0] // 2
        return partial_rows[:half] + swap(partial_rows[half:].astype(BF)).astype(F32)
    return lax.psum_scatter(
        partial_rows.astype(BF), "tensor", scatter_dimension=0, tiled=True
    ).astype(F32)


def lane_of(shape):
    return lax.broadcasted_iota(jnp.int32, shape, 1)


def head_lanes(value, head, spare):
    lane = lane_of(value.shape)
    mine = (lane >= head * HEAD_DIM) & (lane < (head + 1) * HEAD_DIM)
    slot = lane == (1 - head) * HEAD_DIM
    return jnp.where(mine, value, jnp.where(slot, spare, 0.0)).astype(BF)


def positions(count, axis, shape, start, shift, total):
    pos = lax.broadcasted_iota(jnp.int32, shape, axis) + (start + shift)
    return jnp.where(pos >= total, pos - total, pos)


def masked_keys(meta_ref, k_ref, kh_ref):
    total = k_ref.shape[0]
    keys = k_ref[...].astype(F32)
    pos = positions(total, 0, keys.shape, 0, meta_ref[0], total)
    spare = jnp.where(pos < meta_ref[1], 0.0, NEG)
    for head in range(2):
        kh_ref[head] = head_lanes(keys, head, spare)


def scores_of(meta_ref, kh_ref, head, query_f32, start, causal):
    total = kh_ref.shape[1]
    scores = dot(kh_ref[head], head_lanes(query_f32, head, 1.0), 1, 1)
    if causal:
        shape = scores.shape
        key_pos = positions(total, 0, (total, 1), 0, meta_ref[0], total)
        query_pos = positions(shape[1], 1, (1, shape[1]), start, meta_ref[0], total)
        scores = jnp.where(key_pos <= query_pos, scores, NEG)
    return scores


def forward_kernel(meta_ref, q_ref, k_ref, v_ref, ctx_ref, lse_ref, kh_ref, vt_ref, *, causal):
    block = pl.program_id(1)

    @pl.when(block == 0)
    def _():
        masked_keys(meta_ref, k_ref, kh_ref)
        vt_ref[...] = v_ref[...].astype(F32).T.astype(BF)

    query = q_ref[...].astype(F32)
    start = block * q_ref.shape[0]
    parts = []
    for head in range(2):
        scores = scores_of(meta_ref, kh_ref, head, query, start, causal)
        top = jnp.max(scores, axis=0, keepdims=True) * log2_scale
        weights = jnp.exp2(scores * log2_scale - top)
        total = jnp.sum(weights, axis=0, keepdims=True)
        values = vt_ref[head * HEAD_DIM : (head + 1) * HEAD_DIM, :]
        parts.append(dot(values, weights.astype(BF), 1, 0) / total)
        lse_ref[0, head : head + 1, :] = top + jnp.log2(total)
    ctx_ref[...] = jnp.concatenate(parts, axis=0).T.astype(BF)


def backward_kernel(
    meta_ref,
    q_ref,
    k_ref,
    v_ref,
    do_ref,
    ctx_ref,
    lse_ref,
    dq_ref,
    dk_ref,
    dv_ref,
    kh_ref,
    kt_ref,
    dk_acc,
    dv_acc,
    *,
    causal,
):
    block = pl.program_id(1)

    @pl.when(block == 0)
    def _():
        masked_keys(meta_ref, k_ref, kh_ref)
        kt_ref[...] = k_ref[...].astype(F32).T.astype(BF)
        dk_acc[...] = jnp.zeros_like(dk_acc)
        dv_acc[...] = jnp.zeros_like(dv_acc)

    query = q_ref[...].astype(F32)
    grad = do_ref[...].astype(F32)
    start = block * q_ref.shape[0]
    products = (grad * ctx_ref[...].astype(F32)).T
    parts = []
    for head in range(2):
        low, high = head * HEAD_DIM, (head + 1) * HEAD_DIM
        scores = scores_of(meta_ref, kh_ref, head, query, start, causal)
        soft = jnp.exp2(scores * log2_scale - lse_ref[0, head : head + 1, :])
        grad_head = head_lanes(grad, head, 0.0)
        row_dot = jnp.sum(products[low:high, :], axis=0, keepdims=True)
        grad_soft = dot(v_ref[...], grad_head, 1, 1)
        grad_scores = (soft * (grad_soft - row_dot)).astype(BF)
        dv_acc[...] += dot(soft.astype(BF), grad_head, 1, 0)
        dk_acc[...] += dot(grad_scores, head_lanes(query, head, 0.0), 1, 0)
        parts.append(dot(kt_ref[low:high, :], grad_scores, 1, 0))
    dq_ref[...] = (jnp.concatenate(parts, axis=0).T * score_scale).astype(BF)

    @pl.when(block == pl.num_programs(1) - 1)
    def _():
        dk_ref[...] = (dk_acc[...] * score_scale).astype(BF)
        dv_ref[...] = dv_acc[...].astype(BF)


def row_spec(rows):
    return pl.BlockSpec((rows, PAIR), lambda pair, block, meta: (block, pair))


def whole_spec(rows):
    return pl.BlockSpec((rows, PAIR), lambda pair, block, meta: (0, pair))


def lse_spec(rows):
    return pl.BlockSpec((1, 2, rows), lambda pair, block, meta: (pair, 0, block))


def attend_forward(meta, queries, keys, values, causal):
    total, width = queries.shape
    pairs = width // PAIR
    rows = min(QBLK, total)
    return pl.pallas_call(
        partial(forward_kernel, causal=causal),
        grid_spec=pltpu.PrefetchScalarGridSpec(
            num_scalar_prefetch=1,
            grid=(pairs, total // rows),
            in_specs=[row_spec(rows), whole_spec(total), whole_spec(total)],
            out_specs=[row_spec(rows), lse_spec(rows)],
            scratch_shapes=[pltpu.VMEM((2, total, PAIR), BF), pltpu.VMEM((PAIR, total), BF)],
        ),
        out_shape=[
            jax.ShapeDtypeStruct((total, width), BF),
            jax.ShapeDtypeStruct((pairs, 2, total), F32),
        ],
        name="attend_forward",
    )(meta, queries, keys, values)


def attend_backward(meta, queries, keys, values, grad, context, log_sums, causal):
    total, width = queries.shape
    pairs = width // PAIR
    rows = min(QBLK_BACK, total)
    return pl.pallas_call(
        partial(backward_kernel, causal=causal),
        grid_spec=pltpu.PrefetchScalarGridSpec(
            num_scalar_prefetch=1,
            grid=(pairs, total // rows),
            in_specs=[
                row_spec(rows),
                whole_spec(total),
                whole_spec(total),
                row_spec(rows),
                row_spec(rows),
                lse_spec(rows),
            ],
            out_specs=[row_spec(rows), whole_spec(total), whole_spec(total)],
            scratch_shapes=[
                pltpu.VMEM((2, total, PAIR), BF),
                pltpu.VMEM((PAIR, total), BF),
                pltpu.VMEM((total, PAIR), F32),
                pltpu.VMEM((total, PAIR), F32),
            ],
        ),
        out_shape=[jax.ShapeDtypeStruct((total, width), BF)] * 3,
        name="attend_backward",
    )(meta, queries, keys, values, grad, context, log_sums)


def attention_forward(query_in, memory_in, w_qkv, w_out, meta, causal):
    queries = project(query_in, w_qkv[0]).astype(BF)
    keys = project(memory_in, w_qkv[1]).astype(BF)
    values = project(memory_in, w_qkv[2]).astype(BF)
    context, log_sums = attend_forward(meta, queries, keys, values, causal)
    return (collect(project(context, w_out)), (queries, keys, values, context, log_sums))


def attention_backward(
    grad_out, query_in, memory_in, w_qkv, w_out, kept, meta, causal, ticks, name
):
    queries, keys, values, context, log_sums = kept
    grad_full = ticks.mark(name + "_rows", spread(grad_out.astype(BF)))
    grad_context = back_project(grad_full, w_out).astype(BF)
    grad_w_out = weight_grad(grad_full, context).astype(BF)
    grad_q, grad_k, grad_v = attend_backward(
        meta, queries, keys, values, grad_context, context, log_sums, causal
    )
    grad_q = ticks.mark(name + "_kernel", grad_q)
    weight_grads = (
        weight_grad(query_in, grad_q).astype(BF),
        weight_grad(memory_in, grad_k).astype(BF),
        weight_grad(memory_in, grad_v).astype(BF),
        grad_w_out,
    )
    from_query = back_project(grad_q, w_qkv[0])
    from_memory = back_project(grad_k, w_qkv[1]) + back_project(grad_v, w_qkv[2])
    return (weight_grads, from_query, from_memory)


def ffn_forward(normed_rows, w_in, w_out):
    rows_full = spread(normed_rows)
    zed = project(rows_full, w_in)
    unit = gelu_value(zed).astype(BF)
    result = collect(project(unit, w_out))
    return (result, (rows_full, zed, unit, w_in, w_out))


def ffn_backward(grad_out, kept, ticks, name):
    rows, zed, unit, w_in, w_out = kept
    grad_full = ticks.mark(name + "_rows", spread(grad_out.astype(BF)))
    grad_w_out = weight_grad(unit, grad_full).astype(BF)
    grad_unit = back_project(grad_full, w_out).astype(BF)
    grad_zed = (grad_unit.astype(F32) * gelu_slope(zed)).astype(BF)
    grad_zed = ticks.mark(name + "_zed", grad_zed)
    grad_w_in = weight_grad(rows, grad_zed).astype(BF)
    grad_input = collect(back_project(grad_zed, w_in))
    return (grad_input, (grad_w_in, grad_w_out))


def partner(value, bit):
    count = lax.axis_size("dp")
    return lax.ppermute(value, "dp", [(at, at ^ (1 << bit)) for at in range(count)])


class Ticks:
    def __init__(self):
        self.last = lax.axis_index("dp") * 0
        self.marks = {}

    def mark(self, name, value):
        self.last, value = lax.optimization_barrier((self.last, value))
        self.marks[name] = self.last
        return value


def sum_over_pairs(low, high, first_bits, waits):
    levels = lax.axis_size("dp").bit_length() - 1
    order = list(first_bits) + [bit for bit in range(levels) if bit not in first_bits]
    waits = list(waits) + [0] * (2 * levels - len(waits))
    place = lax.axis_index("dp")
    upper = {bit: (place >> bit) & 1 for bit in order}
    send = jnp.where(upper[order[0]] == 1, low, high)
    at = upper[order[0]] + waits[0] == 1
    summed = jnp.where(at, high, low) + partner(send, order[0])
    for bit, wait in zip(order[1:], waits[1:levels]):
        halves = summed.reshape(2, summed.shape[0] // 2, summed.shape[1])
        send = lax.dynamic_index_in_dim(halves, 1 - upper[bit], 0, keepdims=False)
        keep = lax.dynamic_index_in_dim(halves, upper[bit] + wait, 0, keepdims=False)
        summed = keep + partner(send, bit)
    for bit, wait in zip(order[::-1], waits[levels:]):
        other = partner(summed, bit)
        at = upper[bit] + wait == 1
        halves = (jnp.where(at, other, summed), jnp.where(at, summed, other))
        if bit != order[0]:
            summed = jnp.concatenate(halves)
    return (halves[0].astype(F32), halves[1].astype(F32))


def sum_rows(value, first_bits, waits):
    half = value.shape[0] // 2
    return jnp.concatenate(sum_over_pairs(value[:half], value[half:], first_bits, waits))


def sum_ffn(pair, waits=()):
    return (sum_rows(pair[0], (0, 1), waits), sum_rows(pair[1], (1, 0), waits))


def sum_attention(grads, waits=()):
    query, key, value, out = grads
    query, key = sum_over_pairs(query, key, (0, 1), waits)
    value, out = sum_over_pairs(value, out, (1, 0), waits)
    return (jnp.stack([query, key, value]), out.T)


def sum_everywhere(value):
    for axis in ("tensor", "dp"):
        count = lax.axis_size(axis)
        for bit in range(count.bit_length() - 1):
            value = value + lax.ppermute(
                value, axis, [(at, at ^ (1 << bit)) for at in range(count)]
            )
    return value


def on_device(
    src,
    tgt,
    src_len,
    tgt_len,
    enc_qkv,
    enc_out_w,
    enc_ffn_in,
    enc_ffn_out,
    enc_gain,
    enc_bias,
    dec_qkv,
    dec_self_out,
    dec_cross,
    dec_cross_out,
    dec_ffn_in,
    dec_ffn_out,
    dec_gain,
    dec_bias,
    enc_cot,
    dec_cot,
):
    if lax.axis_size("tensor") == 2:
        shift = (lax.axis_index("tensor") * src.shape[1]).astype(jnp.int32)
    else:
        shift = jnp.zeros((), jnp.int32)
    src_meta = jnp.stack([shift, src_len[0]])
    tgt_meta = jnp.stack([shift, tgt_len[0]])
    source = src[0].astype(F32)
    target = tgt[0].astype(F32)
    ln_a1, nm_a1, inv_a1 = norm_forward(source, enc_gain[0], enc_bias[0])
    ln_b1, nm_b1, inv_b1 = norm_forward(target, dec_gain[0], dec_bias[0])
    enc_rows = spread(ln_a1.astype(BF))
    dec_rows = spread(ln_b1.astype(BF))
    attn_enc, keep_enc_attn = attention_forward(
        enc_rows, enc_rows, enc_qkv, enc_out_w, src_meta, False
    )
    hidden_one = source + attn_enc
    ln_a2, nm_a2, inv_a2 = norm_forward(hidden_one, enc_gain[1], enc_bias[1])
    ffn_enc, keep_enc_ffn = ffn_forward(ln_a2.astype(BF), enc_ffn_in, enc_ffn_out)
    hidden_two = hidden_one + ffn_enc
    ln_mem, nm_mem, inv_mem = norm_forward(hidden_two, enc_gain[2], enc_bias[2])
    memory = ln_mem.astype(BF)
    attn_self, keep_self = attention_forward(
        dec_rows, dec_rows, dec_qkv, dec_self_out, tgt_meta, True
    )
    resid_one = target + attn_self
    ln_b2, nm_b2, inv_b2 = norm_forward(resid_one, dec_gain[1], dec_bias[1])
    cross_rows = spread(ln_b2.astype(BF))
    memory_rows = spread(memory)
    attn_cross, keep_cross = attention_forward(
        cross_rows, memory_rows, dec_cross, dec_cross_out, src_meta, False
    )
    resid_two = resid_one + attn_cross
    ln_b3, nm_b3, inv_b3 = norm_forward(resid_two, dec_gain[2], dec_bias[2])
    ffn_dec, keep_dec_ffn = ffn_forward(ln_b3.astype(BF), dec_ffn_in, dec_ffn_out)
    resid_three = resid_two + ffn_dec
    ln_final, nm_final, inv_final = norm_forward(resid_three, dec_gain[3], dec_bias[3])
    ticks = Ticks()
    grad_r3, gain_final, bias_final = norm_backward(
        dec_cot[0].astype(F32), nm_final, inv_final, dec_gain[3]
    )
    grad_b3, dec_ffn_grads = ffn_backward(grad_r3, keep_dec_ffn, ticks, "dec_ffn")
    part_r2, gain_b3, bias_b3 = norm_backward(grad_b3, nm_b3, inv_b3, dec_gain[2])
    grad_r2 = grad_r3 + part_r2
    cross_grads, from_query, from_memory = attention_backward(
        grad_r2,
        cross_rows,
        memory_rows,
        dec_cross,
        dec_cross_out,
        keep_cross,
        src_meta,
        False,
        ticks,
        "cross",
    )
    grad_memory = enc_cot[0].astype(F32) + collect(from_memory)
    grad_h2, gain_mem, bias_mem = norm_backward(grad_memory, nm_mem, inv_mem, enc_gain[2])
    grad_a2, enc_ffn_grads = ffn_backward(grad_h2, keep_enc_ffn, ticks, "enc_ffn")
    part_r1, gain_b2, bias_b2 = norm_backward(collect(from_query), nm_b2, inv_b2, dec_gain[1])
    grad_r1 = grad_r2 + part_r1
    self_grads, self_query, self_memory = attention_backward(
        grad_r1,
        dec_rows,
        dec_rows,
        dec_qkv,
        dec_self_out,
        keep_self,
        tgt_meta,
        True,
        ticks,
        "self",
    )
    grad_b1 = collect(self_query + self_memory)
    part_tgt, gain_b1, bias_b1 = norm_backward(grad_b1, nm_b1, inv_b1, dec_gain[0])
    grad_tgt = grad_r1 + part_tgt
    part_h1, gain_a2, bias_a2 = norm_backward(grad_a2, nm_a2, inv_a2, enc_gain[1])
    grad_h1 = grad_h2 + part_h1
    enc_grads, enc_query, enc_memory = attention_backward(
        grad_h1,
        enc_rows,
        enc_rows,
        enc_qkv,
        enc_out_w,
        keep_enc_attn,
        src_meta,
        False,
        ticks,
        "enc",
    )
    grad_a1 = collect(enc_query + enc_memory)
    part_src, gain_a1, bias_a1 = norm_backward(grad_a1, nm_a1, inv_a1, enc_gain[0])
    grad_src = grad_h1 + part_src
    marks = ticks.marks
    early = (
        marks["cross_kernel"],
        marks["enc_ffn_rows"],
        marks["enc_ffn_zed"],
        marks["self_rows"],
        marks["self_kernel"],
        marks["enc_rows"],
        marks["enc_kernel"],
    )
    dec_ffn_sums = sum_ffn(dec_ffn_grads, early)
    cross_sums = sum_attention(cross_grads, early[3:])
    enc_ffn_sums = sum_ffn(enc_ffn_grads, early[5:])
    self_sums = sum_attention(self_grads, early[6:])
    enc_sums = sum_attention(enc_grads)
    small = sum_everywhere(
        jnp.stack(
            [
                gain_a1,
                gain_a2,
                gain_mem,
                bias_a1,
                bias_a2,
                bias_mem,
                gain_b1,
                gain_b2,
                gain_b3,
                gain_final,
                bias_b1,
                bias_b2,
                bias_b3,
                bias_final,
            ]
        )
    )
    return (
        memory[None],
        ln_final.astype(BF)[None],
        grad_src[None],
        grad_tgt[None],
        enc_sums[0],
        enc_sums[1],
        enc_ffn_sums[0],
        enc_ffn_sums[1],
        small[0:3],
        small[3:6],
        self_sums[0],
        self_sums[1],
        cross_sums[0],
        cross_sums[1],
        dec_ffn_sums[0],
        dec_ffn_sums[1],
        small[6:10],
        small[10:14],
    )


def solution(mesh):
    rows = P("dp", "tensor", None)
    triple = P(None, None, "tensor")
    in_specs = (
        rows,
        rows,
        P("dp"),
        P("dp"),
        triple,
        P("tensor", None),
        P(None, "tensor"),
        P("tensor", None),
        P(),
        P(),
        triple,
        P("tensor", None),
        triple,
        P("tensor", None),
        P(None, "tensor"),
        P("tensor", None),
        P(),
        P(),
        rows,
        rows,
    )
    out_specs = (
        rows,
        rows,
        rows,
        rows,
        triple,
        P("tensor", None),
        P(None, "tensor"),
        P("tensor", None),
        P(),
        P(),
        triple,
        P("tensor", None),
        triple,
        P("tensor", None),
        P(None, "tensor"),
        P("tensor", None),
        P(),
        P(),
    )
    return jax.shard_map(
        on_device, mesh=mesh, in_specs=in_specs, out_specs=out_specs, check_vma=False
    )
```
